512 devices in a mesh: dp: 16 (over x_hi, y, core), seq: 32 (over x_lo, z).
Axes of the slice: x: 4 (x_hi: 2, x_lo: 2; x = x_hi * 2 + x_lo), y: 4, z: 16, core: 2. Of those that a mesh axis runs over, the one named last changes fastest.
Arguments:
- queries: bfloat16 [16, 32768, 128], P('dp', 'seq'), may hold values from -6 to 6
- key_vectors: bfloat16 [16, 32768, 128], P('dp', 'seq'), may hold values from -6 to 6
- value_vectors: bfloat16 [16, 32768, 128], P('dp', 'seq'), may hold values from -6 to 6
- out_grad: bfloat16 [16, 32768, 128], P('dp', 'seq'), may hold values from -6 to 6
- log_decay: float32 [16, 1, 32768], P('dp', None, 'seq'), may hold values from -0.8 to 0, as said below
- prev_grads: bfloat16 [16, 1024, 6144], P('dp', 'seq'), may hold values from -6 to 6
Outputs:
- attn_out: bfloat16 [16, 32768, 128], P('dp', 'seq')
- grad_query: bfloat16 [16, 32768, 128], P('dp', 'seq')
- grad_key: bfloat16 [16, 32768, 128], P('dp', 'seq')
- grad_value: bfloat16 [16, 32768, 128], P('dp', 'seq')
- grad_shard: float32 [1024, 6144], P('seq', 'dp')
The draws below stay inside these ranges and needn't reach their ends.
Inputs may be any that keep to these rules, and one draw needn't show every extreme that they name: `log_decay`: every entry is negative.
All inputs are finite; a program needn't handle non-finite values.
Results may differ from the reference program's by a relative error of at most 0.012.
Values may be sent and summed in bfloat16 or wider, within the bound.
A program may use at most 64 MiB of HBM per device.

```python
import math
import jax
import jax.numpy as jnp
from jax import lax

D = 6144
HEAD_DIM = 128
HEADS = 1
BLK = 512
TOK_DEV = 1024
SEQUENCE_TOKENS = 32768
GR_ROWS = 1024
N_DP = 16


def draw_log_decay(key, part):
    random_key_array = jax.random.split(key, 7)
    flat_ids = jnp.arange(N_DP * HEADS).reshape(N_DP, HEADS)
    keeper_id = jax.random.randint(random_key_array[0], (), 0, N_DP * HEADS)
    coin_flags = jax.random.randint(random_key_array[1], (N_DP, HEADS), 0, 2) == 1
    fast_flags = coin_flags & (flat_ids != keeper_id)
    base_rate = jnp.where(fast_flags, 1.0 / 40.0, math.log(2.0) / SEQUENCE_TOKENS)[:, :, None]
    span_count = SEQUENCE_TOKENS // TOK_DEV
    span_scale = jnp.exp(jax.random.uniform(random_key_array[2], (N_DP, HEADS, span_count), minval=math.log(0.5), maxval=math.log(2.0)))
    span_scale = jnp.repeat(span_scale, TOK_DEV, axis=2)
    roughness = jax.random.uniform(random_key_array[3], (N_DP, HEADS, SEQUENCE_TOKENS), minval=0.5, maxval=1.5)
    decay_rates = -(base_rate * span_scale * roughness)
    first_spot = jax.random.randint(random_key_array[4], (N_DP,), 0, SEQUENCE_TOKENS)
    spot_gap = jax.random.randint(random_key_array[6], (N_DP,), 1, SEQUENCE_TOKENS)
    second_spot = (first_spot + spot_gap) % SEQUENCE_TOKENS
    spike_locations = jnp.stack([first_spot, second_spot], axis=1)
    spike_retained = jax.random.uniform(random_key_array[5], (N_DP, 2), minval=0.5, maxval=0.8)
    token_offsets = jnp.arange(SEQUENCE_TOKENS)[None, None, :]
    spike_matches = (token_offsets == spike_locations[:, :, None]).astype(jnp.float32)
    decay_spikes = jnp.sum(spike_matches * jnp.log(spike_retained)[:, :, None], axis=1)
    return (decay_rates + decay_spikes[:, None, :]).astype(jnp.float32)


def spiked(entries, stream_key, source, target, blocks, factor):
    owner, partner = [(jnp.arange(entries.shape[dim]) // (entries.shape[dim] // blocks)).reshape([-1 if axis == dim else 1 for axis in range(entries.ndim)]) for dim in (source, target)]
    chosen = jax.random.permutation(stream_key, blocks)[partner]
    strong = (owner == chosen) | (owner == (partner + blocks // 2) % blocks)
    return jnp.where(strong, factor * entries, entries)


def shard_levels(key, dims, shards, least, high):
    def one(dim, blocks):
        heights = jax.random.uniform(jax.random.fold_in(jax.random.fold_in(key, 6), dim), (blocks,), jnp.float32, least / len(shards), high / len(shards))
        return jnp.repeat(jnp.exp(heights), dims[dim] // blocks).reshape((-1,) + (1,) * (len(dims) - dim - 1))

    loudness = one(*shards[0])
    for cut in shards[1:]:
        loudness = loudness * one(*cut)
    return loudness


def centred(own_key, dims, width, limit, shards=(), kind=jnp.bfloat16):
    entries = width * jax.random.normal(own_key, dims, jnp.float32)
    if shards:
        entries = entries * shard_levels(own_key, dims, shards, -0.22, 0.18)
    return jnp.clip(entries, -limit, limit).astype(kind)


def noise_with(key, extent, scale, most, shards, heavy, kind=jnp.bfloat16):
    drawn = scale * jax.random.normal(key, extent, jnp.float32)
    if shards:
        drawn = drawn * shard_levels(key, extent, shards, -0.22, 0.18)
    return jnp.clip(spiked(drawn, jax.random.fold_in(key, 3), *heavy), -most, most).astype(kind)


def setup_inputs(seed: int = 0) -> dict:
    keys = jax.random.split(jax.random.key(seed), 7)
    queries = centred(keys[0], (N_DP, SEQUENCE_TOKENS, HEADS * HEAD_DIM), 1.0, 6.0, ((0, 16), (1, 32)))
    key_vectors = centred(keys[1], (N_DP, SEQUENCE_TOKENS, HEADS * HEAD_DIM), 1.0, 6.0, ((0, 16), (1, 32)))
    value_vectors = centred(keys[2], (N_DP, SEQUENCE_TOKENS, HEADS * HEAD_DIM), 1.0, 6.0, ((0, 16), (1, 32)))
    out_grad = centred(keys[3], (N_DP, SEQUENCE_TOKENS, HEADS * HEAD_DIM), 1.0, 6.0, ((0, 16), (1, 32)))
    log_decay = draw_log_decay(jax.random.fold_in(keys[6], 71), 0)
    prev_grads = noise_with(keys[5], (N_DP, GR_ROWS, D), 1.0, 6.0, ((0, 16), (1, 32)), (0, 2, 16, 2.0))
    return dict(queries=queries, key_vectors=key_vectors, value_vectors=value_vectors, out_grad=out_grad, log_decay=log_decay, prev_grads=prev_grads)


NORM_EPS = 1e-06
FULL_PRECISION = lax.Precision.HIGHEST

def product(left, right):
    return jnp.dot(left, right, precision=FULL_PRECISION, preferred_element_type=jnp.float32)

def decay_mask(running):
    spread = running[:, None] - running[None, :]
    lower_mask = jnp.tril(jnp.ones(spread.shape, dtype=bool))
    return jnp.where(lower_mask, jnp.exp(jnp.minimum(spread, 0.0)), 0.0)

def attend(query_rows, key_rows, value_rows, decay_rows):
    block_count = query_rows.shape[0] // BLK
    head_width = query_rows.shape[1]

    def advance(carried, block_inputs):
        query_block, key_block, value_block, decay_block = block_inputs
        running = jnp.cumsum(decay_block)
        scores = product(query_block, key_block.T) * decay_mask(running)
        block_out = product(scores, value_block) + jnp.exp(running)[:, None] * product(query_block, carried)
        weights = jnp.exp(running[-1] - running)
        updated = jnp.exp(running[-1]) * carried + product((key_block * weights[:, None]).T, value_block)
        return (updated, block_out)
    inputs = (query_rows.reshape(block_count, BLK, head_width), key_rows.reshape(block_count, BLK, head_width), value_rows.reshape(block_count, BLK, head_width), decay_rows.reshape(block_count, BLK))
    final_state, outputs = lax.scan(advance, jnp.zeros((head_width, head_width), jnp.float32), inputs)
    return outputs.reshape(block_count * BLK, head_width)

def reference(queries, key_vectors, value_vectors, out_grad, log_decay, prev_grads):
    head_count = log_decay.shape[1]

    def by_head(tensor):
        shaped = tensor.reshape(N_DP, SEQUENCE_TOKENS, head_count, HEAD_DIM).transpose(0, 2, 1, 3)
        return shaped.reshape(N_DP * head_count, SEQUENCE_TOKENS, HEAD_DIM).astype(jnp.float32)

    def to_rows(tensor):
        shaped = tensor.reshape(N_DP, head_count, SEQUENCE_TOKENS, HEAD_DIM).transpose(0, 2, 1, 3)
        return shaped.reshape(N_DP, SEQUENCE_TOKENS, head_count * HEAD_DIM).astype(jnp.bfloat16)
    items = (by_head(queries), by_head(key_vectors), by_head(value_vectors), by_head(out_grad), log_decay.reshape(N_DP * head_count, SEQUENCE_TOKENS))

    def per_item(item):
        query_rows, key_rows, value_rows, cotangent, decay_rows = item

        def forward(query_in, key_in, value_in):
            attention = attend(query_in, key_in, value_in, decay_rows)
            norm_ratio = lax.rsqrt(lax.optimization_barrier(jnp.mean(attention * attention, axis=-1, keepdims=True)) + NORM_EPS)
            return attention * norm_ratio
        normed, pullback = jax.vjp(forward, query_rows, key_rows, value_rows)
        grad_q, grad_k, grad_v = pullback(cotangent)
        return (normed, grad_q, grad_k, grad_v)
    normed, grad_q, grad_k, grad_v = lax.map(per_item, items)
    grad_shard = lax.optimization_barrier(jnp.sum(prev_grads.astype(jnp.float32), axis=0))
    return (to_rows(normed), to_rows(grad_q), to_rows(grad_k), to_rows(grad_v), grad_shard)
```

```python
import functools

import jax
import jax.numpy as jnp
from jax import lax
from jax.experimental import pallas as pl
from jax.experimental.pallas import tpu as pltpu
from jax.sharding import PartitionSpec as P

NORM_EPS = 1e-06
MESH = pl.DeviceIdType.MESH
EXACT = lax.Precision.HIGHEST
F32 = jnp.float32
BF16 = jnp.bfloat16

ROWS = 256
LANES = 128
X_PARTS = 2
QUAD = 4
PIECES = X_PARTS * QUAD


def dot(left, right, left_dim=1, right_dim=0):
    return lax.dot_general(
        left, right, (((left_dim,), (right_dim,)), ((), ())), preferred_element_type=F32
    )


def wait_bytes(ref, sem):
    pltpu.make_async_copy(ref, ref, sem).wait()


def kernel(
    n_dp, n_seq,
    q_hbm, k_hbm, v_hbm, dy_hbm, ld_hbm, pg_hbm,
    out_hbm, gq_hbm, gk_hbm, gv_hbm, gs_hbm,
    q, k, v, dy, ld, out, gq, gk, gv, gs,
    col, lead, tail, mask, scores, keyed, attn, dattn, gkl, gvl,
    state, gathered, prefix, incoming, state2, gathered2, prefix2, outgoing,
    own_log, logs, parts,
    load_sem, store_sem, part_send, part_recv, log_send, log_recv, own_sem,
    s1_send, s1_recv, s2_send, s2_recv, r1_send, r1_recv, r2_send, r2_recv,
):
    tokens, width = q.shape
    blocks = tokens // ROWS
    chunks = tokens // LANES
    n_z = n_seq // X_PARTS
    half = n_z // 2
    my_dp = lax.axis_index("dp")
    me = lax.axis_index("seq")
    my_x = me // n_z
    my_z = me % n_z
    my_quad = my_z // QUAD
    my_piece = my_x * QUAD + my_z % QUAD
    shard = gs.shape[1]

    def member(quad, piece):
        return (piece // QUAD) * n_z + quad * QUAD + piece % QUAD

    def piece_of(device):
        return (device // n_z) * QUAD + (device % n_z) % QUAD

    barrier = pltpu.get_barrier_semaphore()

    @pl.loop(1, n_seq)
    def _(step):
        pl.semaphore_signal(
            barrier, inc=1, device_id=(my_dp, (me + step) % n_seq), device_id_type=MESH
        )

    @pl.loop(1, n_dp)
    def _(step):
        pl.semaphore_signal(
            barrier, inc=1, device_id=((my_dp + step) % n_dp, me), device_id_type=MESH
        )

    loads = [
        pltpu.make_async_copy(source, target, load_sem.at[index])
        for index, (source, target) in enumerate(
            ((ld_hbm, ld), (k_hbm.at[0], k), (v_hbm.at[0], v), (q_hbm.at[0], q), (dy_hbm.at[0], dy))
        )
    ]
    for load in loads:
        load.start()

    loads[0].wait()
    lane_row = lax.broadcasted_iota(jnp.int32, (LANES, LANES), 0)
    lane_col = lax.broadcasted_iota(jnp.int32, (LANES, LANES), 1)
    upper = jnp.where(lane_row <= lane_col, 1.0, 0.0).astype(F32)
    log_rows = ld[...]
    within = jnp.dot(log_rows, upper, precision=EXACT, preferred_element_type=F32)
    totals = jnp.dot(
        log_rows, jnp.ones((LANES, LANES), F32), precision=EXACT, preferred_element_type=F32
    )
    chunk_row = lax.broadcasted_iota(jnp.int32, (chunks, LANES), 0)
    before = jnp.zeros((chunks, LANES), F32)
    for chunk in range(chunks - 1):
        before = before + jnp.where(chunk_row > chunk, totals[chunk : chunk + 1, :], 0.0)
    cum8 = within + before
    whole = before[chunks - 1 : chunks, :] + totals[chunks - 1 : chunks, :]
    own_log[...] = whole
    turned = cum8.T
    for chunk in range(chunks):
        span = pl.ds(chunk * LANES, LANES)
        wide = jnp.broadcast_to(turned[:, chunk : chunk + 1], (LANES, LANES))
        col[span, :] = wide
        tail[span, :] = jnp.exp(jnp.minimum(whole - wide, 0.0))

    loads[1].wait()
    loads[2].wait()
    keyed[...] = (k[...].astype(F32) * tail[...]).astype(BF16)
    local_state = dot(keyed[...], v[...], 0, 0)
    for piece in range(PIECES):
        state[piece] = local_state[piece * 16 : (piece + 1) * 16, :].astype(BF16)

    pl.semaphore_wait(barrier, n_seq - 1 + n_dp - 1)

    def spread(step, other_x):
        offset = jnp.where(step % 2 == 1, half - (step + 1) // 2, half + step // 2)
        target_x = (my_x + other_x) % X_PARTS
        return target_x * n_z + (my_z + offset) % n_z

    def to_owners(source, target, send, recv, with_log):
        def one(step, other_x):
            device = spread(step, other_x)
            if with_log:
                pltpu.make_async_remote_copy(
                    own_log, logs.at[me], log_send, log_recv,
                    device_id=(my_dp, device), device_id_type=MESH,
                ).start()
            pltpu.make_async_remote_copy(
                source.at[piece_of(device)], target.at[me], send, recv,
                device_id=(my_dp, device), device_id_type=MESH,
            ).start()

        @pl.loop(0, n_z - 1)
        def _(step):
            one(step, 1)
            one(step, 0)

        one(n_z - 1, 1)
        if with_log:
            pltpu.make_async_copy(own_log, logs.at[me], log_recv).start()
        pltpu.make_async_copy(source.at[my_piece], target.at[me], recv).start()

    def to_members(source, target, send, recv):
        @pl.loop(1, PIECES)
        def _(step):
            device = member(my_quad, (my_piece + step) % PIECES)
            pltpu.make_async_remote_copy(
                source.at[device], target.at[my_piece], send, recv,
                device_id=(my_dp, device), device_id_type=MESH,
            ).start()

        pltpu.make_async_copy(source.at[me], target.at[my_piece], recv).start()

    to_owners(state, gathered, s1_send, s1_recv, True)

    def columns(device):
        return pl.ds(pl.multiple_of(device * shard, LANES), shard)

    @pl.loop(1, n_dp)
    def _(step):
        device = (my_dp + step) % n_dp
        pltpu.make_async_remote_copy(
            pg_hbm.at[0, :, columns(device)], parts.at[my_dp], part_send, part_recv,
            device_id=(device, me), device_id_type=MESH,
        ).start()

    pltpu.make_async_copy(pg_hbm.at[0, :, columns(my_dp)], parts.at[my_dp], part_recv).start()

    loads[3].wait()
    loads[4].wait()
    lead[...] = jnp.exp(col[...])
    keyed[...] = (q[...].astype(F32) * lead[...]).astype(BF16)
    for block in range(blocks):
        rows = pl.ds(block * ROWS, ROWS)
        col_block = col[rows, :]
        for chunk in range((block + 1) * ROWS // LANES):
            at = pl.ds(chunk * LANES, LANES)
            weights = jnp.exp(jnp.minimum(col_block - cum8[chunk : chunk + 1, :], 0.0))
            if (chunk + 1) * LANES > block * ROWS:
                row_id = lax.broadcasted_iota(jnp.int32, (ROWS, LANES), 0) + block * ROWS
                col_id = lax.broadcasted_iota(jnp.int32, (ROWS, LANES), 1) + chunk * LANES
                weights = jnp.where(row_id >= col_id, weights, 0.0)
            mask[rows, at] = weights
        seen = (block + 1) * ROWS
        scores[rows, :seen] = (dot(q[rows, :], k[:seen, :], 1, 1) * mask[rows, :seen]).astype(BF16)
        attn[rows, :] = dot(scores[rows, :seen], v[:seen, :])

    def scan(order, source, target):
        decays = [jnp.exp(logs[device]) for device in range(n_seq)]
        total = jnp.zeros(source.shape[1:], F32)
        for device in order:
            target[device] = total.astype(BF16)
            total = total * decays[device] + source[device].astype(F32)

    wait_bytes(logs, log_recv)
    wait_bytes(gathered, s1_recv)
    scan(range(n_seq), gathered, prefix)
    to_members(prefix, incoming, s2_send, s2_recv)
    wait_bytes(incoming, s2_recv)

    start_state = incoming[...].reshape(width, width)
    for block in range(blocks):
        rows = pl.ds(block * ROWS, ROWS)
        full = attn[rows, :] + lead[rows, :] * dot(q[rows, :], start_state)
        square = jnp.sum(full * full, axis=1, keepdims=True) * (1.0 / width)
        ratio = lax.rsqrt(square + NORM_EPS)
        cotangent = dy[rows, :].astype(F32)
        along = jnp.sum(cotangent * full, axis=1, keepdims=True)
        normed = full * ratio
        out[rows, :] = normed.astype(BF16)
        dattn[rows, :] = (
            ratio * cotangent - (ratio * ratio * along * (1.0 / width)) * normed
        ).astype(BF16)

    local_future = dot(keyed[...], dattn[...], 0, 0)
    for piece in range(PIECES):
        state2[piece] = local_future[piece * 16 : (piece + 1) * 16, :].astype(BF16)
    to_owners(state2, gathered2, r1_send, r1_recv, False)
    out_store = pltpu.make_async_copy(out, out_hbm.at[0], store_sem.at[0])
    out_store.start()

    for block in range(blocks):
        rows = pl.ds(block * ROWS, ROWS)
        seen = (block + 1) * ROWS
        dscores = (dot(dattn[rows, :], v[:seen, :], 1, 1) * mask[rows, :seen]).astype(BF16)
        gq[rows, :] = (
            dot(dscores, k[:seen, :]) + lead[rows, :] * dot(dattn[rows, :], start_state, 1, 1)
        ).astype(BF16)
        key_part = dot(dscores, q[rows, :], 0, 0)
        value_part = dot(scores[rows, :seen], dattn[rows, :], 0, 0)
        old = block * ROWS
        if block:
            gkl[:old, :] = gkl[:old, :] + key_part[:old, :]
            gvl[:old, :] = gvl[:old, :] + value_part[:old, :]
        gkl[rows, :] = key_part[old:, :]
        gvl[rows, :] = value_part[old:, :]
    gq_store = pltpu.make_async_copy(gq, gq_hbm.at[0], store_sem.at[1])
    gq_store.start()

    wait_bytes(gathered2, r1_recv)
    scan(range(n_seq - 1, -1, -1), gathered2, prefix2)
    to_members(prefix2, outgoing, r2_send, r2_recv)

    wait_bytes(parts, part_recv)
    summed = parts[0].astype(F32)
    for device in range(1, n_dp):
        summed = summed + parts[device].astype(F32)
    gs[...] = summed
    gs_store = pltpu.make_async_copy(gs, gs_hbm, store_sem.at[2])
    gs_store.start()

    wait_bytes(outgoing, r2_recv)
    later = outgoing[...].reshape(width, width)
    stores = [out_store, gq_store, gs_store]
    for block in range(blocks):
        rows = pl.ds(block * ROWS, ROWS)
        fade = tail[rows, :]
        gk[rows, :] = (gkl[rows, :] + fade * dot(v[rows, :], later, 1, 1)).astype(BF16)
        gv[rows, :] = (gvl[rows, :] + fade * dot(k[rows, :], later)).astype(BF16)
    for index, (source, target) in enumerate(((gk, gk_hbm), (gv, gv_hbm))):
        store = pltpu.make_async_copy(source, target.at[0], store_sem.at[3 + index])
        store.start()
        stores.append(store)

    others = n_seq - 1
    wait_bytes(logs.at[pl.ds(0, others)], log_send)
    wait_bytes(gathered.at[pl.ds(0, others)], s1_send)
    wait_bytes(gathered2.at[pl.ds(0, others)], r1_send)
    wait_bytes(incoming.at[pl.ds(0, PIECES - 1)], s2_send)
    wait_bytes(outgoing.at[pl.ds(0, PIECES - 1)], r2_send)
    wait_bytes(parts.at[pl.ds(0, n_dp - 1)], part_send)
    for store in stores:
        store.wait()


def local(n_dp, n_seq, queries, key_vectors, value_vectors, out_grad, log_decay, prev_grads):
    tokens, width = queries.shape[1:]
    grad_rows, grad_cols = prev_grads.shape[1:]
    shard = grad_cols // n_dp
    chunks = tokens // LANES
    wide = jax.ShapeDtypeStruct((1, tokens, width), BF16)
    rows16 = pltpu.VMEM((tokens, width), BF16)
    rows32 = pltpu.VMEM((tokens, width), F32)
    pieces = pltpu.VMEM((PIECES, width // PIECES, width), BF16)
    gather = pltpu.VMEM((n_seq, width // PIECES, width), BF16)
    dma = pltpu.SemaphoreType.DMA
    outs = pl.pallas_call(
        functools.partial(kernel, n_dp, n_seq),
        out_shape=(wide, wide, wide, wide, jax.ShapeDtypeStruct((grad_rows, shard), F32)),
        in_specs=[pl.BlockSpec(memory_space=pl.ANY)] * 6,
        out_specs=[pl.BlockSpec(memory_space=pl.ANY)] * 5,
        scratch_shapes=[
            rows16, rows16, rows16, rows16,
            pltpu.VMEM((chunks, LANES), F32),
            rows16, rows16, rows16, rows16,
            pltpu.VMEM((grad_rows, shard), F32),
            rows32, rows32, rows32,
            pltpu.VMEM((tokens, tokens), F32),
            pltpu.VMEM((tokens, tokens), BF16),
            rows16, rows32, rows16, rows32, rows32,
            pieces, gather, gather, pieces, pieces, gather, gather, pieces,
            pltpu.VMEM((1, LANES), F32),
            pltpu.VMEM((n_seq, 1, LANES), F32),
            pltpu.VMEM((n_dp, grad_rows, shard), BF16),
            dma((5,)), dma((5,)),
        ]
        + [dma(())] * 5
        + [dma(())] * 8,
        compiler_params=pltpu.CompilerParams(collective_id=0, has_side_effects=True),
        name="attention",
    )(
        queries, key_vectors, value_vectors, out_grad,
        log_decay.reshape(chunks, LANES), prev_grads,
    )
    return tuple(outs)


def solution(mesh):
    return jax.shard_map(
        functools.partial(local, mesh.shape["dp"], mesh.shape["seq"]),
        mesh=mesh,
        in_specs=(
            P("dp", "seq", None),
            P("dp", "seq", None),
            P("dp", "seq", None),
            P("dp", "seq", None),
            P("dp", None, "seq"),
            P("dp", "seq", None),
        ),
        out_specs=(
            P("dp", "seq", None),
            P("dp", "seq", None),
            P("dp", "seq", None),
            P("dp", "seq", None),
            P("seq", "dp"),
        ),
        check_vma=False,
    )
```

```python
import functools

import jax
import jax.numpy as jnp
from jax import lax
from jax.experimental import pallas as pl
from jax.experimental.pallas import tpu as pltpu
from jax.sharding import PartitionSpec as P

NORM_EPS = 1e-06
MESH = pl.DeviceIdType.MESH
EXACT = lax.Precision.HIGHEST
F32 = jnp.float32
BF16 = jnp.bfloat16

ROWS = 256
LANES = 128
X_PARTS = 2
QUAD = 4
PIECES = X_PARTS * QUAD


def dot(left, right, left_dim=1, right_dim=0):
    return lax.dot_general(
        left, right, (((left_dim,), (right_dim,)), ((), ())), preferred_element_type=F32
    )


def wait_bytes(ref, sem):
    pltpu.make_async_copy(ref, ref, sem).wait()


def kernel(
    n_dp, n_seq,
    q_hbm, k_hbm, v_hbm, dy_hbm, ld_hbm, pg_hbm,
    k, v, tail, gkl, gvl, outgoing, out, gq, gs,
    q, dy, ld, col, lead, mask, scores, keyed, attn, dattn,
    state, gathered, prefix, incoming, state2, gathered2, prefix2,
    own_log, logs, parts,
    load_sem, part_send, part_recv, log_send, log_recv,
    s1_send, s1_recv, s2_send, s2_recv, r1_send, r1_recv, r2_send, r2_recv,
):
    tokens, width = q.shape
    blocks = tokens // ROWS
    chunks = tokens // LANES
    n_z = n_seq // X_PARTS
    half = n_z // 2
    my_dp = lax.axis_index("dp")
    me = lax.axis_index("seq")
    my_x = me // n_z
    my_z = me % n_z
    my_quad = my_z // QUAD
    my_piece = my_x * QUAD + my_z % QUAD
    shard = gs.shape[1]

    def member(quad, piece):
        return (piece // QUAD) * n_z + quad * QUAD + piece % QUAD

    barrier = pltpu.get_barrier_semaphore()

    def each_far_first(one):
        other_x = X_PARTS - 1 - my_x

        def pair(z):
            one(other_x, z)
            one(my_x, z)

        pair(lax.rem(my_z + half, n_z))

        @pl.loop(1, half)
        def _(step):
            pair(lax.rem(my_z + half - step, n_z))
            pair(lax.rem(my_z + half + step, n_z))

        one(other_x, my_z)

    def greet(x, z):
        pl.semaphore_signal(
            barrier, inc=1, device_id=(my_dp, x * n_z + z), device_id_type=MESH
        )

    each_far_first(greet)

    @pl.loop(1, n_dp)
    def _(step):
        pl.semaphore_signal(
            barrier, inc=1, device_id=(lax.rem(my_dp + step, n_dp), me), device_id_type=MESH
        )

    loads = [
        pltpu.make_async_copy(source, target, load_sem.at[index])
        for index, (source, target) in enumerate(
            ((ld_hbm, ld), (k_hbm.at[0], k), (v_hbm.at[0], v), (q_hbm.at[0], q), (dy_hbm.at[0], dy))
        )
    ]
    for load in loads:
        load.start()

    loads[0].wait()
    lane_row = lax.broadcasted_iota(jnp.int32, (LANES, LANES), 0)
    lane_col = lax.broadcasted_iota(jnp.int32, (LANES, LANES), 1)
    upper = jnp.where(lane_row <= lane_col, 1.0, 0.0).astype(F32)
    log_rows = ld[...]
    within = jnp.dot(log_rows, upper, precision=EXACT, preferred_element_type=F32)
    totals = jnp.dot(
        log_rows, jnp.ones((LANES, LANES), F32), precision=EXACT, preferred_element_type=F32
    )
    chunk_row = lax.broadcasted_iota(jnp.int32, (chunks, LANES), 0)
    before = jnp.zeros((chunks, LANES), F32)
    for chunk in range(chunks - 1):
        before = before + jnp.where(chunk_row > chunk, totals[chunk : chunk + 1, :], 0.0)
    cum8 = within + before
    whole = before[chunks - 1 : chunks, :] + totals[chunks - 1 : chunks, :]
    own_log[...] = whole
    turned = cum8.T
    for chunk in range(chunks):
        span = pl.ds(chunk * LANES, LANES)
        wide = jnp.broadcast_to(turned[:, chunk : chunk + 1], (LANES, LANES))
        col[span, :] = wide
        tail[span, :] = jnp.exp(jnp.minimum(whole - wide, 0.0))

    loads[1].wait()
    loads[2].wait()
    keyed[...] = (k[...].astype(F32) * tail[...]).astype(BF16)
    local_state = dot(keyed[...], v[...], 0, 0)
    for piece in range(PIECES):
        state[piece] = local_state[piece * 16 : (piece + 1) * 16, :].astype(BF16)

    pl.semaphore_wait(barrier, n_seq - 1 + n_dp - 1)

    quads = n_z // QUAD

    def to_owners(source, target, send, recv, forward):
        free = my_x == (0 if forward else X_PARTS - 1)
        slot = jnp.where(free, 0, my_quad + 1)

        def one(x, z):
            device = (my_dp, x * n_z + z)
            quad = z // QUAD
            if forward:
                pltpu.make_async_remote_copy(
                    own_log, logs.at[me], log_send, log_recv,
                    device_id=device, device_id_type=MESH,
                ).start()
            needed = quad >= my_quad if forward else quad <= my_quad

            @pl.when(free | needed)
            def _():
                pltpu.make_async_remote_copy(
                    source.at[x * QUAD + lax.rem(z, QUAD)], target.at[me],
                    send.at[quad], recv.at[slot],
                    device_id=device, device_id_type=MESH,
                ).start()

        each_far_first(one)
        if forward:
            pltpu.make_async_copy(own_log, logs.at[me], log_recv).start()
        pltpu.make_async_copy(source.at[my_piece], target.at[me], recv.at[slot]).start()

    def owners_sent(target, send, forward):
        free = my_x == (0 if forward else X_PARTS - 1)
        for quad in range(quads):
            needed = my_quad <= quad if forward else my_quad >= quad

            @pl.when((free | needed) & (my_quad != quad))
            def _():
                wait_bytes(target.at[pl.ds(0, PIECES)], send.at[quad])

            @pl.when(my_quad == quad)
            def _():
                wait_bytes(target.at[pl.ds(0, PIECES - 1)], send.at[quad])

    def owners_received(target, recv, forward):
        free = 0 if forward else X_PARTS - 1
        wait_bytes(target.at[pl.ds(free * n_z, n_z)], recv.at[0])
        for quad in range(quads):

            @pl.when(my_quad >= quad if forward else my_quad <= quad)
            def _():
                wait_bytes(
                    target.at[pl.ds((X_PARTS - 1 - free) * n_z + quad * QUAD, QUAD)],
                    recv.at[quad + 1],
                )

    def to_members(source, target, send, recv):
        @pl.loop(1, PIECES)
        def _(step):
            device = member(my_quad, lax.rem(my_piece + step, PIECES))
            pltpu.make_async_remote_copy(
                source.at[device], target.at[my_piece], send, recv,
                device_id=(my_dp, device), device_id_type=MESH,
            ).start()

        pltpu.make_async_copy(source.at[me], target.at[my_piece], recv).start()

    to_owners(state, gathered, s1_send, s1_recv, True)

    def columns(device):
        return pl.ds(pl.multiple_of(device * shard, LANES), shard)

    @pl.loop(1, n_dp)
    def _(step):
        device = lax.rem(my_dp + step, n_dp)
        pltpu.make_async_remote_copy(
            pg_hbm.at[0, :, columns(device)], parts.at[my_dp], part_send, part_recv,
            device_id=(device, me), device_id_type=MESH,
        ).start()

    pltpu.make_async_copy(pg_hbm.at[0, :, columns(my_dp)], parts.at[my_dp], part_recv).start()

    loads[3].wait()
    loads[4].wait()
    lead[...] = jnp.exp(col[...])
    keyed[...] = (q[...].astype(F32) * lead[...]).astype(BF16)
    for block in range(blocks):
        rows = pl.ds(block * ROWS, ROWS)
        col_block = col[rows, :]
        for chunk in range((block + 1) * ROWS // LANES):
            at = pl.ds(chunk * LANES, LANES)
            weights = jnp.exp(jnp.minimum(col_block - cum8[chunk : chunk + 1, :], 0.0))
            if (chunk + 1) * LANES > block * ROWS:
                row_id = lax.broadcasted_iota(jnp.int32, (ROWS, LANES), 0) + block * ROWS
                col_id = lax.broadcasted_iota(jnp.int32, (ROWS, LANES), 1) + chunk * LANES
                weights = jnp.where(row_id >= col_id, weights, 0.0)
            mask[rows, at] = weights
        seen = (block + 1) * ROWS
        scores[rows, :seen] = (dot(q[rows, :], k[:seen, :], 1, 1) * mask[rows, :seen]).astype(BF16)
        attn[rows, :] = dot(scores[rows, :seen], v[:seen, :])

    def scan(order, source, target):
        decays = [jnp.exp(logs[device]) for device in range(n_seq)]
        total = jnp.zeros(source.shape[1:], F32)
        for device in order:
            target[device] = total.astype(BF16)
            total = total * decays[device] + source[device].astype(F32)

    wait_bytes(logs, log_recv)
    owners_received(gathered, s1_recv, True)
    scan(range(n_seq), gathered, prefix)
    to_members(prefix, incoming, s2_send, s2_recv)
    wait_bytes(incoming, s2_recv)

    start_state = incoming[...].reshape(width, width)
    for block in range(blocks):
        rows = pl.ds(block * ROWS, ROWS)
        full = attn[rows, :] + lead[rows, :] * dot(q[rows, :], start_state)
        square = jnp.sum(full * full, axis=1, keepdims=True) * (1.0 / width)
        ratio = lax.rsqrt(square + NORM_EPS)
        cotangent = dy[rows, :].astype(F32)
        along = jnp.sum(cotangent * full, axis=1, keepdims=True)
        normed = full * ratio
        out[rows, :] = normed.astype(BF16)
        dattn[rows, :] = (
            ratio * cotangent - (ratio * ratio * along * (1.0 / width)) * normed
        ).astype(BF16)

    local_future = dot(keyed[...], dattn[...], 0, 0)
    for piece in range(PIECES):
        state2[piece] = local_future[piece * 16 : (piece + 1) * 16, :].astype(BF16)
    to_owners(state2, gathered2, r1_send, r1_recv, False)

    for block in range(blocks):
        rows = pl.ds(block * ROWS, ROWS)
        seen = (block + 1) * ROWS
        dscores = (dot(dattn[rows, :], v[:seen, :], 1, 1) * mask[rows, :seen]).astype(BF16)
        gq[rows, :] = (
            dot(dscores, k[:seen, :]) + lead[rows, :] * dot(dattn[rows, :], start_state, 1, 1)
        ).astype(BF16)
        key_part = dot(dscores, q[rows, :], 0, 0)
        value_part = dot(scores[rows, :seen], dattn[rows, :], 0, 0)
        old = block * ROWS
        if block:
            gkl[:old, :] = gkl[:old, :] + key_part[:old, :]
            gvl[:old, :] = gvl[:old, :] + value_part[:old, :]
        gkl[rows, :] = key_part[old:, :]
        gvl[rows, :] = value_part[old:, :]

    owners_received(gathered2, r1_recv, False)
    scan(range(n_seq - 1, -1, -1), gathered2, prefix2)
    to_members(prefix2, outgoing, r2_send, r2_recv)

    wait_bytes(parts, part_recv)
    summed = parts[0].astype(F32)
    for device in range(1, n_dp):
        summed = summed + parts[device].astype(F32)
    gs[...] = summed

    wait_bytes(outgoing, r2_recv)

    others = n_seq - 1
    wait_bytes(logs.at[pl.ds(0, others)], log_send)
    owners_sent(gathered, s1_send, True)
    owners_sent(gathered2, r1_send, False)
    wait_bytes(incoming.at[pl.ds(0, PIECES - 1)], s2_send)
    wait_bytes(outgoing.at[pl.ds(0, PIECES - 1)], r2_send)
    wait_bytes(parts.at[pl.ds(0, n_dp - 1)], part_send)


def finish(
    k, v, tail, gkl, gvl, outgoing, out, gq, gs,
    out_hbm, gq_hbm, gk_hbm, gv_hbm, gs_hbm,
    gk, gv, early_sem, late_sem,
):
    tokens, width = k.shape
    blocks = tokens // ROWS
    stores = [
        pltpu.make_async_copy(source, target, early_sem.at[index])
        for index, (source, target) in enumerate(
            ((out, out_hbm.at[0]), (gq, gq_hbm.at[0]), (gs, gs_hbm))
        )
    ]
    for store in stores:
        store.start()
    later = outgoing[...].reshape(width, width)
    for block in range(blocks):
        rows = pl.ds(block * ROWS, ROWS)
        fade = tail[rows, :]
        gk[rows, :] = (gkl[rows, :] + fade * dot(v[rows, :], later, 1, 1)).astype(BF16)
        gv[rows, :] = (gvl[rows, :] + fade * dot(k[rows, :], later)).astype(BF16)
        for index, (source, target) in enumerate(((gk, gk_hbm), (gv, gv_hbm))):
            store = pltpu.make_async_copy(
                source.at[rows], target.at[0, rows], late_sem.at[2 * block + index]
            )
            store.start()
            stores.append(store)
    for store in stores:
        store.wait()


def local(n_dp, n_seq, queries, key_vectors, value_vectors, out_grad, log_decay, prev_grads):
    tokens, width = queries.shape[1:]
    grad_rows, grad_cols = prev_grads.shape[1:]
    shard = grad_cols // n_dp
    chunks = tokens // LANES
    quads = n_seq // PIECES
    wide = jax.ShapeDtypeStruct((1, tokens, width), BF16)
    rows16 = pltpu.VMEM((tokens, width), BF16)
    rows32 = pltpu.VMEM((tokens, width), F32)
    pieces = pltpu.VMEM((PIECES, width // PIECES, width), BF16)
    gather = pltpu.VMEM((n_seq, width // PIECES, width), BF16)
    dma = pltpu.SemaphoreType.DMA
    held = (
        rows16, rows16, rows32, rows32, rows32, pieces, rows16, rows16,
        pltpu.VMEM((grad_rows, shard), F32),
    )
    middle = pl.pallas_call(
        functools.partial(kernel, n_dp, n_seq),
        out_shape=held,
        in_specs=[pl.BlockSpec(memory_space=pltpu.HBM)] * 6,
        out_specs=[pl.BlockSpec(memory_space=pltpu.VMEM)] * len(held),
        scratch_shapes=[
            rows16, rows16,
            pltpu.VMEM((chunks, LANES), F32),
            rows32, rows32,
            pltpu.VMEM((tokens, tokens), F32),
            pltpu.VMEM((tokens, tokens), BF16),
            rows16, rows32, rows16,
            pieces, gather, gather, pieces, pieces, gather, gather,
            pltpu.VMEM((1, LANES), F32),
            pltpu.VMEM((n_seq, 1, LANES), F32),
            pltpu.VMEM((n_dp, grad_rows, shard), BF16),
            dma((5,)),
        ]
        + [dma(())] * 4
        + [dma((quads,)), dma((quads + 1,)), dma(()), dma(())] * 2,
        compiler_params=pltpu.CompilerParams(
            collective_id=0, has_side_effects=True, vmem_limit_bytes=32 * 1024 * 1024
        ),
        name="attention",
    )(
        *(
            pltpu.with_memory_space_constraint(array, pltpu.HBM)
            for array in (
                queries, key_vectors, value_vectors, out_grad,
                log_decay.reshape(chunks, LANES), prev_grads,
            )
        )
    )
    outs = pl.pallas_call(
        finish,
        out_shape=(wide, wide, wide, wide, jax.ShapeDtypeStruct((grad_rows, shard), F32)),
        in_specs=[pl.BlockSpec(memory_space=pltpu.VMEM)] * len(held),
        out_specs=[pl.BlockSpec(memory_space=pl.ANY)] * 5,
        scratch_shapes=[rows16, rows16, dma((3,)), dma((2 * (tokens // ROWS),))],
        compiler_params=pltpu.CompilerParams(vmem_limit_bytes=8 * 1024 * 1024),
        name="finish",
    )(*middle)
    return tuple(outs)


def solution(mesh):
    return jax.shard_map(
        functools.partial(local, mesh.shape["dp"], mesh.shape["seq"]),
        mesh=mesh,
        in_specs=(
            P("dp", "seq", None),
            P("dp", "seq", None),
            P("dp", "seq", None),
            P("dp", "seq", None),
            P("dp", None, "seq"),
            P("dp", "seq", None),
        ),
        out_specs=(
            P("dp", "seq", None),
            P("dp", "seq", None),
            P("dp", "seq", None),
            P("dp", "seq", None),
            P("seq", "dp"),
        ),
        check_vma=False,
    )
```

```python
import functools

import jax
import jax.numpy as jnp
from jax import lax
from jax.experimental import pallas as pl
from jax.experimental.pallas import tpu as pltpu
from jax.sharding import PartitionSpec as P

NORM_EPS = 1e-06
MESH = pl.DeviceIdType.MESH
EXACT = lax.Precision.HIGHEST
F32 = jnp.float32
BF16 = jnp.bfloat16

ROWS = 256
LANES = 128
X_PARTS = 2
QUAD = 4
PIECES = X_PARTS * QUAD


def dot(left, right, left_dim=1, right_dim=0):
    return lax.dot_general(
        left, right, (((left_dim,), (right_dim,)), ((), ())), preferred_element_type=F32
    )


def wait_bytes(ref, sem):
    pltpu.make_async_copy(ref, ref, sem).wait()


def kernel(
    n_dp, n_seq,
    q_hbm, k_hbm, v_hbm, dy_hbm, ld_hbm, pg_hbm,
    k, v, tail, gkl, gvl, outgoing, out, gq, gs,
    q, dy, ld, col, lead, mask, scores, keyed, attn, dattn,
    state, gathered, prefix, incoming, state2, gathered2, prefix2,
    own_log, logs, parts,
    load_sem, part_send, part_recv, log_send, log_recv,
    s1_send, s1_recv, s2_send, s2_recv, r1_send, r1_recv, r2_send, r2_recv,
):
    tokens, width = q.shape
    blocks = tokens // ROWS
    chunks = tokens // LANES
    n_z = n_seq // X_PARTS
    half = n_z // 2
    my_dp = lax.axis_index("dp")
    side = lax.rem(my_dp, 2)
    owning = side == 1
    owner_dp = my_dp + 1 - side
    me = lax.axis_index("seq")
    my_x = me // n_z
    my_z = me % n_z
    my_quad = my_z // QUAD
    my_piece = my_x * QUAD + my_z % QUAD
    shard = gs.shape[1]

    def member(quad, piece):
        return (piece // QUAD) * n_z + quad * QUAD + piece % QUAD

    barrier = pltpu.get_barrier_semaphore()

    def each_far_first(one):
        other_x = X_PARTS - 1 - my_x

        def pair(z):
            one(other_x, z)
            one(my_x, z)

        pair(lax.rem(my_z + half, n_z))

        @pl.loop(1, half)
        def _(step):
            pair(lax.rem(my_z + half - step, n_z))
            pair(lax.rem(my_z + half + step, n_z))

        one(other_x, my_z)

    def greet(dp, device):
        pl.semaphore_signal(barrier, inc=1, device_id=(dp, device), device_id_type=MESH)

    @pl.when(owning)
    def _():
        def both(x, z):
            greet(my_dp - 1, x * n_z + z)
            greet(my_dp, x * n_z + z)

        each_far_first(both)
        greet(my_dp - 1, me)

    @pl.when(jnp.logical_not(owning))
    def _():
        @pl.loop(0, PIECES)
        def _(piece):
            greet(owner_dp, member(my_quad, piece))

    @pl.loop(1, n_dp)
    def _(step):
        pl.semaphore_signal(
            barrier, inc=1, device_id=(lax.rem(my_dp + step, n_dp), me), device_id_type=MESH
        )

    loads = [
        pltpu.make_async_copy(source, target, load_sem.at[index])
        for index, (source, target) in enumerate(
            ((ld_hbm, ld), (k_hbm.at[0], k), (v_hbm.at[0], v), (q_hbm.at[0], q), (dy_hbm.at[0], dy))
        )
    ]
    for load in loads:
        load.start()

    loads[0].wait()
    lane_row = lax.broadcasted_iota(jnp.int32, (LANES, LANES), 0)
    lane_col = lax.broadcasted_iota(jnp.int32, (LANES, LANES), 1)
    upper = jnp.where(lane_row <= lane_col, 1.0, 0.0).astype(F32)
    log_rows = ld[...]
    within = jnp.dot(log_rows, upper, precision=EXACT, preferred_element_type=F32)
    totals = jnp.dot(
        log_rows, jnp.ones((LANES, LANES), F32), precision=EXACT, preferred_element_type=F32
    )
    chunk_row = lax.broadcasted_iota(jnp.int32, (chunks, LANES), 0)
    before = jnp.zeros((chunks, LANES), F32)
    for chunk in range(chunks - 1):
        before = before + jnp.where(chunk_row > chunk, totals[chunk : chunk + 1, :], 0.0)
    cum8 = within + before
    whole = before[chunks - 1 : chunks, :] + totals[chunks - 1 : chunks, :]
    own_log[...] = whole
    turned = cum8.T
    for chunk in range(chunks):
        span = pl.ds(chunk * LANES, LANES)
        wide = jnp.broadcast_to(turned[:, chunk : chunk + 1], (LANES, LANES))
        col[span, :] = wide
        tail[span, :] = jnp.exp(jnp.minimum(whole - wide, 0.0))

    loads[1].wait()
    loads[2].wait()
    keyed[...] = (k[...].astype(F32) * tail[...]).astype(BF16)
    local_state = dot(keyed[...], v[...], 0, 0)
    for piece in range(PIECES):
        state[piece] = local_state[piece * 16 : (piece + 1) * 16, :].astype(BF16)

    pl.semaphore_wait(barrier, n_dp - 1 + jnp.where(owning, n_seq - 1 + PIECES, n_seq))

    quads = n_z // QUAD

    def to_owners(source, target, send, recv, forward):
        free = my_x == (0 if forward else X_PARTS - 1)
        slot = jnp.where(free, 0, my_quad + 1)

        def one(x, z):
            device = (owner_dp, x * n_z + z)
            quad = z // QUAD
            if forward:
                pltpu.make_async_remote_copy(
                    own_log, logs.at[side, me], log_send, log_recv.at[side],
                    device_id=device, device_id_type=MESH,
                ).start()
            needed = quad >= my_quad if forward else quad <= my_quad

            @pl.when(free | needed)
            def _():
                pltpu.make_async_remote_copy(
                    source.at[x * QUAD + lax.rem(z, QUAD)], target.at[side, me],
                    send.at[quad], recv.at[side, slot],
                    device_id=device, device_id_type=MESH,
                ).start()

        each_far_first(one)

        @pl.when(owning)
        def _():
            if forward:
                pltpu.make_async_copy(own_log, logs.at[1, me], log_recv.at[1]).start()
            pltpu.make_async_copy(
                source.at[my_piece], target.at[1, me], recv.at[1, slot]
            ).start()

        @pl.when(jnp.logical_not(owning))
        def _():
            one(my_x, my_z)

    def owners_sent(target, send, forward):
        free = my_x == (0 if forward else X_PARTS - 1)
        for quad in range(quads):
            needed = my_quad <= quad if forward else my_quad >= quad
            short = owning & (my_quad == quad)

            @pl.when((free | needed) & jnp.logical_not(short))
            def _():
                wait_bytes(target.at[0, pl.ds(0, PIECES)], send.at[quad])

            @pl.when(short)
            def _():
                wait_bytes(target.at[0, pl.ds(0, PIECES - 1)], send.at[quad])

    def owners_received(target, recv, forward):
        free = 0 if forward else X_PARTS - 1
        wait_bytes(target.at[pl.ds(free * n_z, n_z)], recv.at[0])
        for quad in range(quads):

            @pl.when(my_quad >= quad if forward else my_quad <= quad)
            def _():
                wait_bytes(
                    target.at[pl.ds((X_PARTS - 1 - free) * n_z + quad * QUAD, QUAD)],
                    recv.at[quad + 1],
                )

    def scan(order, decay_logs, source, target):
        decays = [jnp.exp(decay_logs[device]) for device in range(n_seq)]
        total = jnp.zeros(source.shape[1:], F32)
        for device in order:
            target[device] = total.astype(BF16)
            total = total * decays[device] + source[device].astype(F32)

    def serve(target, recv, pieces, result, member_send, member_recv, forward):
        @pl.when(owning)
        def _():
            for core in (1, 0):
                if forward:
                    wait_bytes(logs.at[core], log_recv.at[core])
                owners_received(target.at[core], recv.at[core], forward)
                order = range(n_seq) if forward else range(n_seq - 1, -1, -1)
                scan(order, logs.at[core], target.at[core], pieces.at[core])
                dp = my_dp - 1 + core

                @pl.loop(1, PIECES)
                def _(step):
                    device = member(my_quad, lax.rem(my_piece + step, PIECES))
                    pltpu.make_async_remote_copy(
                        pieces.at[core, device], result.at[my_piece], member_send, member_recv,
                        device_id=(dp, device), device_id_type=MESH,
                    ).start()

                if core:
                    pltpu.make_async_copy(
                        pieces.at[core, me], result.at[my_piece], member_recv
                    ).start()
                else:
                    pltpu.make_async_remote_copy(
                        pieces.at[core, me], result.at[my_piece], member_send, member_recv,
                        device_id=(dp, me), device_id_type=MESH,
                    ).start()

    to_owners(state, gathered, s1_send, s1_recv, True)

    def columns(device):
        return pl.ds(pl.multiple_of(device * shard, LANES), shard)

    @pl.loop(1, n_dp)
    def _(step):
        device = lax.rem(my_dp + step, n_dp)
        pltpu.make_async_remote_copy(
            pg_hbm.at[0, :, columns(device)], parts.at[my_dp], part_send, part_recv,
            device_id=(device, me), device_id_type=MESH,
        ).start()

    pltpu.make_async_copy(pg_hbm.at[0, :, columns(my_dp)], parts.at[my_dp], part_recv).start()

    loads[3].wait()
    loads[4].wait()
    lead[...] = jnp.exp(col[...])
    keyed[...] = (q[...].astype(F32) * lead[...]).astype(BF16)
    for block in range(blocks):
        rows = pl.ds(block * ROWS, ROWS)
        col_block = col[rows, :]
        for chunk in range((block + 1) * ROWS // LANES):
            at = pl.ds(chunk * LANES, LANES)
            weights = jnp.exp(jnp.minimum(col_block - cum8[chunk : chunk + 1, :], 0.0))
            if (chunk + 1) * LANES > block * ROWS:
                row_id = lax.broadcasted_iota(jnp.int32, (ROWS, LANES), 0) + block * ROWS
                col_id = lax.broadcasted_iota(jnp.int32, (ROWS, LANES), 1) + chunk * LANES
                weights = jnp.where(row_id >= col_id, weights, 0.0)
            mask[rows, at] = weights
        seen = (block + 1) * ROWS
        scores[rows, :seen] = (dot(q[rows, :], k[:seen, :], 1, 1) * mask[rows, :seen]).astype(BF16)
        attn[rows, :] = dot(scores[rows, :seen], v[:seen, :])

    serve(gathered, s1_recv, prefix, incoming, s2_send, s2_recv, True)
    wait_bytes(incoming, s2_recv)

    start_state = incoming[...].reshape(width, width)
    for block in range(blocks):
        rows = pl.ds(block * ROWS, ROWS)
        full = attn[rows, :] + lead[rows, :] * dot(q[rows, :], start_state)
        square = jnp.sum(full * full, axis=1, keepdims=True) * (1.0 / width)
        ratio = lax.rsqrt(square + NORM_EPS)
        cotangent = dy[rows, :].astype(F32)
        along = jnp.sum(cotangent * full, axis=1, keepdims=True)
        normed = full * ratio
        out[rows, :] = normed.astype(BF16)
        dattn[rows, :] = (
            ratio * cotangent - (ratio * ratio * along * (1.0 / width)) * normed
        ).astype(BF16)

    local_future = dot(keyed[...], dattn[...], 0, 0)
    for piece in range(PIECES):
        state2[piece] = local_future[piece * 16 : (piece + 1) * 16, :].astype(BF16)
    to_owners(state2, gathered2, r1_send, r1_recv, False)

    for block in range(blocks):
        rows = pl.ds(block * ROWS, ROWS)
        seen = (block + 1) * ROWS
        dscores = (dot(dattn[rows, :], v[:seen, :], 1, 1) * mask[rows, :seen]).astype(BF16)
        gq[rows, :] = (
            dot(dscores, k[:seen, :]) + lead[rows, :] * dot(dattn[rows, :], start_state, 1, 1)
        ).astype(BF16)
        key_part = dot(dscores, q[rows, :], 0, 0)
        value_part = dot(scores[rows, :seen], dattn[rows, :], 0, 0)
        old = block * ROWS
        if block:
            gkl[:old, :] = gkl[:old, :] + key_part[:old, :]
            gvl[:old, :] = gvl[:old, :] + value_part[:old, :]
        gkl[rows, :] = key_part[old:, :]
        gvl[rows, :] = value_part[old:, :]

    serve(gathered2, r1_recv, prefix2, outgoing, r2_send, r2_recv, False)

    wait_bytes(parts, part_recv)
    summed = parts[0].astype(F32)
    for device in range(1, n_dp):
        summed = summed + parts[device].astype(F32)
    gs[...] = summed

    wait_bytes(outgoing, r2_recv)

    owners_sent(gathered, s1_send, True)
    owners_sent(gathered2, r1_send, False)

    @pl.when(owning)
    def _():
        wait_bytes(logs.at[0, pl.ds(0, n_seq - 1)], log_send)
        sent = pl.ds(0, 2 * PIECES - 1)
        wait_bytes(prefix.at[0, sent], s2_send)
        wait_bytes(prefix2.at[0, sent], r2_send)

    @pl.when(jnp.logical_not(owning))
    def _():
        wait_bytes(logs.at[0], log_send)

    wait_bytes(parts.at[pl.ds(0, n_dp - 1)], part_send)


def finish(
    k, v, tail, gkl, gvl, outgoing, out, gq, gs,
    out_hbm, gq_hbm, gk_hbm, gv_hbm, gs_hbm,
    gk, gv, early_sem, late_sem,
):
    tokens, width = k.shape
    blocks = tokens // ROWS
    stores = [
        pltpu.make_async_copy(source, target, early_sem.at[index])
        for index, (source, target) in enumerate(
            ((out, out_hbm.at[0]), (gq, gq_hbm.at[0]), (gs, gs_hbm))
        )
    ]
    for store in stores:
        store.start()
    later = outgoing[...].reshape(width, width)
    for block in range(blocks):
        rows = pl.ds(block * ROWS, ROWS)
        fade = tail[rows, :]
        gk[rows, :] = (gkl[rows, :] + fade * dot(v[rows, :], later, 1, 1)).astype(BF16)
        gv[rows, :] = (gvl[rows, :] + fade * dot(k[rows, :], later)).astype(BF16)
        for index, (source, target) in enumerate(((gk, gk_hbm), (gv, gv_hbm))):
            store = pltpu.make_async_copy(
                source.at[rows], target.at[0, rows], late_sem.at[2 * block + index]
            )
            store.start()
            stores.append(store)
    for store in stores:
        store.wait()


def local(n_dp, n_seq, queries, key_vectors, value_vectors, out_grad, log_decay, prev_grads):
    tokens, width = queries.shape[1:]
    grad_rows, grad_cols = prev_grads.shape[1:]
    shard = grad_cols // n_dp
    chunks = tokens // LANES
    quads = n_seq // PIECES
    wide = jax.ShapeDtypeStruct((1, tokens, width), BF16)
    rows16 = pltpu.VMEM((tokens, width), BF16)
    rows32 = pltpu.VMEM((tokens, width), F32)
    pieces = pltpu.VMEM((PIECES, width // PIECES, width), BF16)
    gather = pltpu.VMEM((2, n_seq, width // PIECES, width), BF16)
    dma = pltpu.SemaphoreType.DMA
    held = (
        rows16, rows16, rows32, rows32, rows32, pieces, rows16, rows16,
        pltpu.VMEM((grad_rows, shard), F32),
    )
    middle = pl.pallas_call(
        functools.partial(kernel, n_dp, n_seq),
        out_shape=held,
        in_specs=[pl.BlockSpec(memory_space=pltpu.HBM)] * 6,
        out_specs=[pl.BlockSpec(memory_space=pltpu.VMEM)] * len(held),
        scratch_shapes=[
            rows16, rows16,
            pltpu.VMEM((chunks, LANES), F32),
            rows32, rows32,
            pltpu.VMEM((tokens, tokens), F32),
            pltpu.VMEM((tokens, tokens), BF16),
            rows16, rows32, rows16,
            pieces, gather, gather, pieces, pieces, gather, gather,
            pltpu.VMEM((1, LANES), F32),
            pltpu.VMEM((2, n_seq, 1, LANES), F32),
            pltpu.VMEM((n_dp, grad_rows, shard), BF16),
            dma((5,)),
        ]
        + [dma(())] * 3
        + [dma((2,))]
        + [dma((quads,)), dma((2, quads + 1)), dma(()), dma(())] * 2,
        compiler_params=pltpu.CompilerParams(
            collective_id=0, has_side_effects=True, vmem_limit_bytes=32 * 1024 * 1024
        ),
        name="attention",
    )(
        *(
            pltpu.with_memory_space_constraint(array, pltpu.HBM)
            for array in (
                queries, key_vectors, value_vectors, out_grad,
                log_decay.reshape(chunks, LANES), prev_grads,
            )
        )
    )
    outs = pl.pallas_call(
        finish,
        out_shape=(wide, wide, wide, wide, jax.ShapeDtypeStruct((grad_rows, shard), F32)),
        in_specs=[pl.BlockSpec(memory_space=pltpu.VMEM)] * len(held),
        out_specs=[pl.BlockSpec(memory_space=pl.ANY)] * 5,
        scratch_shapes=[rows16, rows16, dma((3,)), dma((2 * (tokens // ROWS),))],
        compiler_params=pltpu.CompilerParams(vmem_limit_bytes=8 * 1024 * 1024),
        name="finish",
    )(*middle)
    return tuple(outs)


def solution(mesh):
    return jax.shard_map(
        functools.partial(local, mesh.shape["dp"], mesh.shape["seq"]),
        mesh=mesh,
        in_specs=(
            P("dp", "seq", None),
            P("dp", "seq", None),
            P("dp", "seq", None),
            P("dp", "seq", None),
            P("dp", None, "seq"),
            P("dp", "seq", None),
        ),
        out_specs=(
            P("dp", "seq", None),
            P("dp", "seq", None),
            P("dp", "seq", None),
            P("dp", "seq", None),
            P("seq", "dp"),
        ),
        check_vma=False,
    )
```

```python
import functools

import jax
import jax.numpy as jnp
from jax import lax
from jax.experimental import pallas as pl
from jax.experimental.pallas import tpu as pltpu
from jax.sharding import PartitionSpec as P

NORM_EPS = 1e-06
MESH = pl.DeviceIdType.MESH
EXACT = lax.Precision.HIGHEST
F32 = jnp.float32
BF16 = jnp.bfloat16

ROWS = 256
LANES = 128
X_PARTS = 2
QUAD = 4
SHIFT = 1
PIECES = X_PARTS * QUAD


def dot(left, right, left_dim=1, right_dim=0):
    return lax.dot_general(
        left, right, (((left_dim,), (right_dim,)), ((), ())), preferred_element_type=F32
    )


def wait_bytes(ref, sem):
    pltpu.make_async_copy(ref, ref, sem).wait()


def kernel(
    n_dp, n_seq,
    q_hbm, k_hbm, v_hbm, dy_hbm, ld_hbm, pg_hbm,
    k, v, tail, gkl, gvl, outgoing, out, gq, gs,
    q, dy, ld, col, lead, mask, scores, keyed, attn, dattn,
    state, gathered, prefix, incoming, state2, gathered2, prefix2,
    own_log, logs, parts,
    load_sem, part_send, part_recv, log_send, log_recv,
    s1_send, s1_recv, s2_send, s2_recv, r1_send, r1_recv, r2_send, r2_recv,
):
    tokens, width = q.shape
    blocks = tokens // ROWS
    chunks = tokens // LANES
    n_z = n_seq // X_PARTS
    half = n_z // 2
    my_dp = lax.axis_index("dp")
    side = lax.rem(my_dp, 2)
    owning = side == 1
    owner_dp = my_dp + 1 - side
    me = lax.axis_index("seq")
    my_x = me // n_z
    my_z = me % n_z
    my_quad = lax.rem(my_z + SHIFT, n_z) // QUAD
    my_piece = my_x * QUAD + lax.rem(my_z + SHIFT, QUAD)
    shard = gs.shape[1]

    def member(quad, piece):
        z = lax.rem(quad * QUAD + lax.rem(piece, QUAD) + n_z - SHIFT, n_z)
        return (piece // QUAD) * n_z + z

    barrier = pltpu.get_barrier_semaphore()

    def each_far_first(one):
        other_x = X_PARTS - 1 - my_x

        def pair(z):
            one(other_x, z)
            one(my_x, z)

        pair(lax.rem(my_z + half, n_z))

        @pl.loop(1, half)
        def _(step):
            pair(lax.rem(my_z + half - step, n_z))
            pair(lax.rem(my_z + half + step, n_z))

        one(other_x, my_z)

    def greet(dp, device):
        pl.semaphore_signal(barrier, inc=1, device_id=(dp, device), device_id_type=MESH)

    @pl.when(owning)
    def _():
        def both(x, z):
            greet(my_dp - 1, x * n_z + z)
            greet(my_dp, x * n_z + z)

        each_far_first(both)
        greet(my_dp - 1, me)

    @pl.when(jnp.logical_not(owning))
    def _():
        @pl.loop(0, PIECES)
        def _(piece):
            greet(owner_dp, member(my_quad, piece))

    @pl.loop(1, n_dp)
    def _(step):
        pl.semaphore_signal(
            barrier, inc=1, device_id=(lax.rem(my_dp + step, n_dp), me), device_id_type=MESH
        )

    loads = [
        pltpu.make_async_copy(source, target, load_sem.at[index])
        for index, (source, target) in enumerate(
            ((ld_hbm, ld), (k_hbm.at[0], k), (v_hbm.at[0], v), (q_hbm.at[0], q), (dy_hbm.at[0], dy))
        )
    ]
    for load in loads:
        load.start()

    loads[0].wait()
    lane_row = lax.broadcasted_iota(jnp.int32, (LANES, LANES), 0)
    lane_col = lax.broadcasted_iota(jnp.int32, (LANES, LANES), 1)
    upper = jnp.where(lane_row <= lane_col, 1.0, 0.0).astype(F32)
    log_rows = ld[...]
    within = jnp.dot(log_rows, upper, precision=EXACT, preferred_element_type=F32)
    totals = jnp.dot(
        log_rows, jnp.ones((LANES, LANES), F32), precision=EXACT, preferred_element_type=F32
    )
    chunk_row = lax.broadcasted_iota(jnp.int32, (chunks, LANES), 0)
    before = jnp.zeros((chunks, LANES), F32)
    for chunk in range(chunks - 1):
        before = before + jnp.where(chunk_row > chunk, totals[chunk : chunk + 1, :], 0.0)
    cum8 = within + before
    whole = before[chunks - 1 : chunks, :] + totals[chunks - 1 : chunks, :]
    own_log[...] = whole
    turned = cum8.T
    for chunk in range(chunks):
        span = pl.ds(chunk * LANES, LANES)
        wide = jnp.broadcast_to(turned[:, chunk : chunk + 1], (LANES, LANES))
        col[span, :] = wide
        tail[span, :] = jnp.exp(jnp.minimum(whole - wide, 0.0))

    loads[1].wait()
    loads[2].wait()
    keyed[...] = (k[...].astype(F32) * tail[...]).astype(BF16)
    local_state = dot(keyed[...], v[...], 0, 0)
    for piece in range(PIECES):
        state[piece] = local_state[piece * 16 : (piece + 1) * 16, :].astype(BF16)

    pl.semaphore_wait(barrier, n_dp - 1 + jnp.where(owning, n_seq - 1 + PIECES, n_seq))

    quads = n_z // QUAD

    def before(source_quad, quad):
        return (source_quad <= quad) | (quad == 0)

    def after(source_quad, quad):
        return (source_quad >= quad) | (source_quad == 0)

    def to_owners(source, target, send, recv, forward):
        free = my_x == (0 if forward else X_PARTS - 1)
        slot = jnp.where(free, 0, my_quad + 1)

        def one(x, z):
            device = (owner_dp, x * n_z + z)
            quad = lax.rem(z + SHIFT, n_z) // QUAD
            if forward:
                pltpu.make_async_remote_copy(
                    own_log, logs.at[side, me], log_send, log_recv.at[side],
                    device_id=device, device_id_type=MESH,
                ).start()
            needed = before(my_quad, quad) if forward else after(my_quad, quad)

            @pl.when(free | needed)
            def _():
                pltpu.make_async_remote_copy(
                    source.at[x * QUAD + lax.rem(z + SHIFT, QUAD)], target.at[side, me],
                    send.at[quad], recv.at[side, slot],
                    device_id=device, device_id_type=MESH,
                ).start()

        each_far_first(one)

        @pl.when(owning)
        def _():
            if forward:
                pltpu.make_async_copy(own_log, logs.at[1, me], log_recv.at[1]).start()
            pltpu.make_async_copy(
                source.at[my_piece], target.at[1, me], recv.at[1, slot]
            ).start()

        @pl.when(jnp.logical_not(owning))
        def _():
            one(my_x, my_z)

    def owners_sent(target, send, forward):
        free = my_x == (0 if forward else X_PARTS - 1)
        for quad in range(quads):
            needed = before(my_quad, quad) if forward else after(my_quad, quad)
            short = owning & (my_quad == quad)

            @pl.when((free | needed) & jnp.logical_not(short))
            def _():
                wait_bytes(target.at[0, pl.ds(0, PIECES)], send.at[quad])

            @pl.when(short)
            def _():
                wait_bytes(target.at[0, pl.ds(0, PIECES - 1)], send.at[quad])

    def owners_received(target, recv, forward):
        free = 0 if forward else X_PARTS - 1
        wait_bytes(target.at[pl.ds(free * n_z, n_z)], recv.at[0])
        for quad in range(quads):

            @pl.when(before(quad, my_quad) if forward else after(quad, my_quad))
            def _():
                wait_bytes(
                    target.at[pl.ds((X_PARTS - 1 - free) * n_z + quad * QUAD, QUAD)],
                    recv.at[quad + 1],
                )

    def scan(order, decay_logs, source, target):
        decays = [jnp.exp(decay_logs[device]) for device in range(n_seq)]
        total = jnp.zeros(source.shape[1:], F32)
        for device in order:
            target[device] = total.astype(BF16)
            total = total * decays[device] + source[device].astype(F32)

    def serve(target, recv, pieces, result, member_send, member_recv, forward):
        @pl.when(owning)
        def _():
            for core in (1, 0):
                if forward:
                    wait_bytes(logs.at[core], log_recv.at[core])
                owners_received(target.at[core], recv.at[core], forward)
                order = range(n_seq) if forward else range(n_seq - 1, -1, -1)
                scan(order, logs.at[core], target.at[core], pieces.at[core])
                dp = my_dp - 1 + core

                @pl.loop(1, PIECES)
                def _(step):
                    device = member(my_quad, lax.rem(my_piece + step, PIECES))
                    pltpu.make_async_remote_copy(
                        pieces.at[core, device], result.at[my_piece], member_send, member_recv,
                        device_id=(dp, device), device_id_type=MESH,
                    ).start()

                if core:
                    pltpu.make_async_copy(
                        pieces.at[core, me], result.at[my_piece], member_recv
                    ).start()
                else:
                    pltpu.make_async_remote_copy(
                        pieces.at[core, me], result.at[my_piece], member_send, member_recv,
                        device_id=(dp, me), device_id_type=MESH,
                    ).start()

    to_owners(state, gathered, s1_send, s1_recv, True)

    def columns(device):
        return pl.ds(pl.multiple_of(device * shard, LANES), shard)

    @pl.loop(1, n_dp)
    def _(step):
        device = lax.rem(my_dp + step, n_dp)
        pltpu.make_async_remote_copy(
            pg_hbm.at[0, :, columns(device)], parts.at[my_dp], part_send, part_recv,
            device_id=(device, me), device_id_type=MESH,
        ).start()

    pltpu.make_async_copy(pg_hbm.at[0, :, columns(my_dp)], parts.at[my_dp], part_recv).start()

    loads[3].wait()
    loads[4].wait()
    lead[...] = jnp.exp(col[...])
    keyed[...] = (q[...].astype(F32) * lead[...]).astype(BF16)
    for block in range(blocks):
        rows = pl.ds(block * ROWS, ROWS)
        col_block = col[rows, :]
        for chunk in range((block + 1) * ROWS // LANES):
            at = pl.ds(chunk * LANES, LANES)
            weights = jnp.exp(jnp.minimum(col_block - cum8[chunk : chunk + 1, :], 0.0))
            if (chunk + 1) * LANES > block * ROWS:
                row_id = lax.broadcasted_iota(jnp.int32, (ROWS, LANES), 0) + block * ROWS
                col_id = lax.broadcasted_iota(jnp.int32, (ROWS, LANES), 1) + chunk * LANES
                weights = jnp.where(row_id >= col_id, weights, 0.0)
            mask[rows, at] = weights
        seen = (block + 1) * ROWS
        scores[rows, :seen] = (dot(q[rows, :], k[:seen, :], 1, 1) * mask[rows, :seen]).astype(BF16)
        attn[rows, :] = dot(scores[rows, :seen], v[:seen, :])

    serve(gathered, s1_recv, prefix, incoming, s2_send, s2_recv, True)
    wait_bytes(incoming, s2_recv)

    start_state = incoming[...].reshape(width, width)
    for block in range(blocks):
        rows = pl.ds(block * ROWS, ROWS)
        full = attn[rows, :] + lead[rows, :] * dot(q[rows, :], start_state)
        square = jnp.sum(full * full, axis=1, keepdims=True) * (1.0 / width)
        ratio = lax.rsqrt(square + NORM_EPS)
        cotangent = dy[rows, :].astype(F32)
        along = jnp.sum(cotangent * full, axis=1, keepdims=True)
        normed = full * ratio
        out[rows, :] = normed.astype(BF16)
        dattn[rows, :] = (
            ratio * cotangent - (ratio * ratio * along * (1.0 / width)) * normed
        ).astype(BF16)

    local_future = dot(keyed[...], dattn[...], 0, 0)
    for piece in range(PIECES):
        state2[piece] = local_future[piece * 16 : (piece + 1) * 16, :].astype(BF16)
    to_owners(state2, gathered2, r1_send, r1_recv, False)

    for block in range(blocks):
        rows = pl.ds(block * ROWS, ROWS)
        seen = (block + 1) * ROWS
        dscores = (dot(dattn[rows, :], v[:seen, :], 1, 1) * mask[rows, :seen]).astype(BF16)
        gq[rows, :] = (
            dot(dscores, k[:seen, :]) + lead[rows, :] * dot(dattn[rows, :], start_state, 1, 1)
        ).astype(BF16)
        key_part = dot(dscores, q[rows, :], 0, 0)
        value_part = dot(scores[rows, :seen], dattn[rows, :], 0, 0)
        old = block * ROWS
        if block:
            gkl[:old, :] = gkl[:old, :] + key_part[:old, :]
            gvl[:old, :] = gvl[:old, :] + value_part[:old, :]
        gkl[rows, :] = key_part[old:, :]
        gvl[rows, :] = value_part[old:, :]

    serve(gathered2, r1_recv, prefix2, outgoing, r2_send, r2_recv, False)

    wait_bytes(parts, part_recv)
    summed = parts[0].astype(F32)
    for device in range(1, n_dp):
        summed = summed + parts[device].astype(F32)
    gs[...] = summed

    owners_sent(gathered, s1_send, True)
    owners_sent(gathered2, r1_send, False)

    @pl.when(owning)
    def _():
        wait_bytes(logs.at[0, pl.ds(0, n_seq - 1)], log_send)
        sent = pl.ds(0, 2 * PIECES - 1)
        wait_bytes(prefix.at[0, sent], s2_send)

    @pl.when(jnp.logical_not(owning))
    def _():
        wait_bytes(logs.at[0], log_send)

    wait_bytes(parts.at[pl.ds(0, n_dp - 1)], part_send)
    wait_bytes(outgoing, r2_recv)

    @pl.when(owning)
    def _():
        wait_bytes(prefix2.at[0, pl.ds(0, 2 * PIECES - 1)], r2_send)


def finish(
    k, v, tail, gkl, gvl, outgoing, out, gq, gs,
    out_hbm, gq_hbm, gk_hbm, gv_hbm, gs_hbm,
    gk, gv, early_sem, late_sem,
):
    tokens, width = k.shape
    blocks = tokens // ROWS
    stores = [
        pltpu.make_async_copy(source, target, early_sem.at[index])
        for index, (source, target) in enumerate(
            ((out, out_hbm.at[0]), (gq, gq_hbm.at[0]), (gs, gs_hbm))
        )
    ]
    for store in stores:
        store.start()
    later = outgoing[...].reshape(width, width)
    for block in range(blocks):
        rows = pl.ds(block * ROWS, ROWS)
        fade = tail[rows, :]
        gk[rows, :] = (gkl[rows, :] + fade * dot(v[rows, :], later, 1, 1)).astype(BF16)
        gv[rows, :] = (gvl[rows, :] + fade * dot(k[rows, :], later)).astype(BF16)
        for index, (source, target) in enumerate(((gk, gk_hbm), (gv, gv_hbm))):
            store = pltpu.make_async_copy(
                source.at[rows], target.at[0, rows], late_sem.at[2 * block + index]
            )
            store.start()
            stores.append(store)
    for store in stores:
        store.wait()


def local(n_dp, n_seq, queries, key_vectors, value_vectors, out_grad, log_decay, prev_grads):
    tokens, width = queries.shape[1:]
    grad_rows, grad_cols = prev_grads.shape[1:]
    shard = grad_cols // n_dp
    chunks = tokens // LANES
    quads = n_seq // PIECES
    wide = jax.ShapeDtypeStruct((1, tokens, width), BF16)
    rows16 = pltpu.VMEM((tokens, width), BF16)
    rows32 = pltpu.VMEM((tokens, width), F32)
    pieces = pltpu.VMEM((PIECES, width // PIECES, width), BF16)
    gather = pltpu.VMEM((2, n_seq, width // PIECES, width), BF16)
    dma = pltpu.SemaphoreType.DMA
    held = (
        rows16, rows16, rows32, rows32, rows32, pieces, rows16, rows16,
        pltpu.VMEM((grad_rows, shard), F32),
    )
    middle = pl.pallas_call(
        functools.partial(kernel, n_dp, n_seq),
        out_shape=held,
        in_specs=[pl.BlockSpec(memory_space=pltpu.HBM)] * 6,
        out_specs=[pl.BlockSpec(memory_space=pltpu.VMEM)] * len(held),
        scratch_shapes=[
            rows16, rows16,
            pltpu.VMEM((chunks, LANES), F32),
            rows32, rows32,
            pltpu.VMEM((tokens, tokens), F32),
            pltpu.VMEM((tokens, tokens), BF16),
            rows16, rows32, rows16,
            pieces, gather, gather, pieces, pieces, gather, gather,
            pltpu.VMEM((1, LANES), F32),
            pltpu.VMEM((2, n_seq, 1, LANES), F32),
            pltpu.VMEM((n_dp, grad_rows, shard), BF16),
            dma((5,)),
        ]
        + [dma(())] * 3
        + [dma((2,))]
        + [dma((quads,)), dma((2, quads + 1)), dma(()), dma(())] * 2,
        compiler_params=pltpu.CompilerParams(
            collective_id=0, has_side_effects=True, vmem_limit_bytes=32 * 1024 * 1024
        ),
        name="attention",
    )(
        *(
            pltpu.with_memory_space_constraint(array, pltpu.HBM)
            for array in (
                queries, key_vectors, value_vectors, out_grad,
                log_decay.reshape(chunks, LANES), prev_grads,
            )
        )
    )
    outs = pl.pallas_call(
        finish,
        out_shape=(wide, wide, wide, wide, jax.ShapeDtypeStruct((grad_rows, shard), F32)),
        in_specs=[pl.BlockSpec(memory_space=pltpu.VMEM)] * len(held),
        out_specs=[pl.BlockSpec(memory_space=pl.ANY)] * 5,
        scratch_shapes=[rows16, rows16, dma((3,)), dma((2 * (tokens // ROWS),))],
        compiler_params=pltpu.CompilerParams(vmem_limit_bytes=8 * 1024 * 1024),
        name="finish",
    )(*middle)
    return tuple(outs)


def solution(mesh):
    return jax.shard_map(
        functools.partial(local, mesh.shape["dp"], mesh.shape["seq"]),
        mesh=mesh,
        in_specs=(
            P("dp", "seq", None),
            P("dp", "seq", None),
            P("dp", "seq", None),
            P("dp", "seq", None),
            P("dp", None, "seq"),
            P("dp", "seq", None),
        ),
        out_specs=(
            P("dp", "seq", None),
            P("dp", "seq", None),
            P("dp", "seq", None),
            P("dp", "seq", None),
            P("seq", "dp"),
        ),
        check_vma=False,
    )
```
